128 devices in a mesh: erow: 8 (over x, core), ecol: 16 (over z, y).
Axes of the slice: x: 4, y: 4, z: 4, core: 2. Of those that a mesh axis runs over, the one named last changes fastest.
Arguments:
- tokens: bfloat16 [1024, 7168], P(('erow', 'ecol')), may hold values from -6 to 6
- routes: int32 [1024, 4], P(('erow', 'ecol')), may hold values from 0 to 15, all different within a row; in each aligned block of 8 rows (0 to 7, 8 to 15, ...) at most 4 rows name the same one
- gate_probs: bfloat16 [1024, 4], P(('erow', 'ecol')), may hold values from 0.049804688 to 0.5
- cotangent: bfloat16 [1024, 7168], P(('erow', 'ecol')), may hold values from -0.625 to 0.625
- w_gate_up: bfloat16 [16, 7168, 2, 2048], P('ecol', 'erow'), may hold values from -0.0625 to 0.0625
- w_down: bfloat16 [16, 2048, 7168], P('ecol', None, 'erow'), may hold values from -0.125 to 0.125
Outputs:
- layer_out: bfloat16 [1024, 7168], P(('erow', 'ecol'))
- grad_tokens: bfloat16 [1024, 7168], P(('erow', 'ecol'))
- grad_probs: float32 [1024, 4], P(('erow', 'ecol'))
- grad_gate_up: bfloat16 [16, 7168, 2, 2048], P('ecol', 'erow')
- grad_down: bfloat16 [16, 2048, 7168], P('ecol', None, 'erow')
The draws below stay inside these ranges and needn't reach their ends.
Inputs may be any that keep to these rules, and one draw needn't show every extreme that they name: `routes`: each row names 4 different experts; among the 8 rows of one device no expert is named more than 4 times, and in some device's rows an expert is named exactly 4 times.
All inputs are finite; a program needn't handle non-finite values.
Results may differ from the reference program's by a relative error of at most 0.039.
Values may be sent and summed in bfloat16 or wider, within the bound.
A program may use at most 128 MiB of HBM per device.

```python
import math
import jax
import jax.numpy as jnp
import numpy as np
from jax import lax

D = 7168
EXPERT_HIDDEN = 2048
TOP_W = 4
TOK_DEV = 8
CAP = 4
EXPERTS = 16
TOKENS = 1024
N_EROW = 8


def block_levels(own_key, shape, shards, smallest, largest):
    level, own = 1.0, jax.random.fold_in(own_key, 6)
    for dim, blocks in shards:
        steps = jnp.exp(jax.random.uniform(jax.random.fold_in(own, dim), (blocks,), jnp.float32, smallest / len(shards), largest / len(shards)))
        level = level * jnp.repeat(steps, shape[dim] // blocks).reshape([-1 if axis == dim else 1 for axis in range(len(shape))])
    return level


def shared_out(own_key, own, number, rows, count, top, limit, slope):
    sequence = jax.random.permutation(own_key, count)
    heavy_load, common = portions_of(count, rows * top, limit, slope, True), portions_of(count, rows * top, limit, slope, False)
    places = jnp.arange(count)

    def named(tallies, turn):
        used = int((tallies > 0).sum())
        fixed = max(1, used // 4)
        moved = fixed + (places - fixed + turn * (used - fixed)) % max(1, count - fixed)
        return jnp.zeros((count,), jnp.int32).at[sequence[jnp.where(places < fixed, places, moved)]].set(jnp.asarray(tallies, jnp.int32))

    tallies = jnp.where(number % 4 == 0, named(heavy_load, number // 4), named(common, number - number // 4 - 1))
    mixed = jax.random.permutation(jax.random.fold_in(own, 3), count)
    donor, taker = mixed[0:count // 2 * 2:2], mixed[1:count // 2 * 2:2]
    margin = jnp.minimum(tallies[donor] - 1, limit - tallies[taker]) // 2
    margin = jnp.where((donor == sequence[0]) | (taker == sequence[0]) | (tallies[taker] == 0), 0, jnp.maximum(margin, 0))
    moved = jax.random.randint(jax.random.fold_in(own, 4), (count // 2,), 0, 1 << 20) % (margin + 1)
    tallies = tallies.at[donor].add(-moved).at[taker].add(moved)
    members = jnp.searchsorted(jnp.cumsum(tallies), jnp.arange(rows * top), side="right").astype(jnp.int32)
    table = members.reshape(top, rows).T
    table = table[jax.random.permutation(jax.random.fold_in(own, 1), rows)]
    turn = jax.random.randint(jax.random.fold_in(own, 2), (rows, 1), 0, top)
    return jnp.take_along_axis(table, (jnp.arange(top)[None, :] + turn) % top, axis=1)


def portions_of(number_of, total, bound, skew, full):
    portions = [(1 << 20) // math.isqrt(rank ** skew) + 1 for rank in range(1, number_of + 1)]
    largest = bound if full else min(bound, max(-(-total // number_of), total * portions[0] // sum(portions)))
    least = 1 if total - largest >= number_of - 1 else 0
    given, surplus = [largest] + [least] * (number_of - 1), total - largest - least * (number_of - 1)
    while surplus > 0:
        free = [i for i in range(1, number_of) if given[i] < largest] or [i for i in range(1, number_of) if given[i] < bound]
        whole, budget = sum([portions[i] for i in free]), surplus
        for i in free:
            more = min(bound - given[i], max(1, budget * portions[i] // whole), surplus)
            given[i] = given[i] + more
            surplus = surplus - more
    return np.array(given)


def gaussian(own_key, extent, deviation, most, shards=(), kind=jnp.bfloat16):
    values = deviation * jax.random.normal(own_key, extent, jnp.float32)
    if shards:
        values = values * block_levels(own_key, extent, shards, -0.22, 0.18)
    return jnp.clip(values, -most, most).astype(kind)


def setup_inputs(seed: int = 0) -> dict:
    key_list = jax.random.split(jax.random.key(seed), 7)
    tokens = gaussian(key_list[0], (TOKENS, D), 1.0, 6.0, ((0, 128),))
    routes_keys = jax.random.split(jax.random.fold_in(key_list[1], 1), TOKENS // TOK_DEV)
    routes_turns = jax.random.permutation(jax.random.fold_in(key_list[1], 3), TOKENS // TOK_DEV)
    routes = jax.vmap(lambda own, number: shared_out(jax.random.fold_in(key_list[1], 2), own, number, TOK_DEV, EXPERTS, TOP_W, CAP, 2))(routes_keys, routes_turns).reshape((TOKENS, TOP_W))
    gate_probs = jnp.clip(jnp.exp(math.log(0.5) - 2.306499 * jax.random.uniform(key_list[2], (TOKENS, TOP_W), jnp.float32) ** block_levels(key_list[2], (TOKENS, TOP_W), ((0, 128),), -0.2, 0.2)), 0.049804688, 0.5).astype(jnp.bfloat16)
    cotangent = gaussian(key_list[3], (TOKENS, D), 0.1, 0.625, ((0, 128),))
    w_gate_up = gaussian(key_list[4], (EXPERTS, D, 2, EXPERT_HIDDEN), D ** -0.5, 0.0625, ((0, 16), (1, 8)))
    w_down = gaussian(key_list[5], (EXPERTS, EXPERT_HIDDEN, D), EXPERT_HIDDEN ** -0.5, 0.125, ((0, 16), (2, 8)))
    return dict(tokens=tokens, routes=routes, gate_probs=gate_probs, cotangent=cotangent, w_gate_up=w_gate_up, w_down=w_down)


def rounded(value):
    return lax.optimization_barrier(value.astype(jnp.bfloat16)).astype(jnp.float32)


def reference(tokens, routes, gate_probs, cotangent, w_gate_up, w_down):
    token_count = tokens.shape[0]
    model_width = tokens.shape[1]
    weight_slice = model_width // N_EROW
    expert_ids = jnp.arange(EXPERTS, dtype=jnp.int32)
    chosen = routes[:, :, None] == expert_ids[None, None, :]
    probs_te = jnp.sum(jnp.where(chosen, gate_probs.astype(jnp.float32)[:, :, None], 0.0), axis=1)
    tokens_f = tokens.astype(jnp.float32)
    token_blocks = tokens_f.reshape(token_count, N_EROW, weight_slice)
    cot_f32 = cotangent.astype(jnp.float32)
    cot_blocks = cot_f32.reshape(token_count, N_EROW, weight_slice)

    def expert_step(totals, inputs):
        out_acc, grad_acc = totals
        w_in, w_out, expert_index = inputs
        prob_col = jnp.sum(jnp.where(expert_ids[None, :] == expert_index, probs_te, 0.0), axis=1)
        w_in_f = w_in.astype(jnp.float32)
        output_weight_float = w_out.astype(jnp.float32)
        parts = jnp.einsum("trd,rdgf->trgf", token_blocks, w_in_f.reshape(N_EROW, weight_slice, 2, EXPERT_HIDDEN))
        pre_sums = jnp.sum(rounded(parts), axis=1)
        gate_pre = pre_sums[:, 0, :]
        up_pre = pre_sums[:, 1, :]
        sigmoid_gate = jax.nn.sigmoid(gate_pre)
        activated = gate_pre * sigmoid_gate
        hidden = (activated * up_pre).astype(jnp.bfloat16)
        expert_out = jnp.dot(hidden, w_out, preferred_element_type=jnp.float32)
        out_acc = out_acc + rounded(prob_col[:, None] * expert_out)
        scaled_cotangent = rounded(prob_col[:, None] * cot_f32)
        dot_parts = jnp.sum(cot_blocks * expert_out.reshape(token_count, N_EROW, weight_slice), axis=2)
        dprob = jnp.sum(rounded(dot_parts), axis=1)
        hidden_pieces = jnp.einsum("kxa,hxa->kxh", scaled_cotangent.reshape(token_count, N_EROW, weight_slice), output_weight_float.reshape(EXPERT_HIDDEN, N_EROW, weight_slice))
        hidden_gradient = jnp.sum(rounded(hidden_pieces), axis=1)
        grad_gate = hidden_gradient * up_pre * sigmoid_gate * (1.0 + gate_pre * (1.0 - sigmoid_gate))
        grad_up = hidden_gradient * activated
        grad_pre = rounded(jnp.stack([grad_gate, grad_up], axis=1))
        grad_rows = rounded(jnp.einsum("tgf,dgf->td", grad_pre, w_in_f))
        grad_acc = grad_acc + grad_rows
        grad_in = jnp.einsum("td,tgf->dgf", tokens_f, grad_pre).astype(jnp.bfloat16)
        grad_out = jnp.einsum("tf,td->fd", hidden.astype(jnp.float32), scaled_cotangent).astype(jnp.bfloat16)
        return (out_acc, grad_acc), (dprob, grad_in, grad_out)

    zeros = jnp.zeros((token_count, model_width), jnp.float32)
    totals, stacked = lax.scan(expert_step, (zeros, zeros), (w_gate_up, w_down, expert_ids))
    dprob_all, grad_gate_up, grad_down = stacked
    grad_probs = jnp.sum(jnp.where(chosen, jnp.transpose(dprob_all)[:, None, :], 0.0), axis=2)
    return (totals[0].astype(jnp.bfloat16), totals[1].astype(jnp.bfloat16), grad_probs, grad_gate_up, grad_down)
```

```python
import jax
import jax.numpy as jnp
from jax import lax
from jax.experimental import pallas as pl
from jax.experimental.pallas import tpu as pltpu
from jax.sharding import PartitionSpec as P

BF = jnp.bfloat16
F32 = jnp.float32
MESH = pl.DeviceIdType.MESH
NX, NK, NZ, NY = 4, 2, 4, 4
NR, NE = NX * NK, NZ * NY
CAP = 4
NQ = 4
OFFSETS = (
    (0, 0), (0, 1), (0, 3), (1, 0),
    (2, 2), (1, 2), (2, 1), (1, 1),
    (3, 2), (2, 3), (3, 3), (2, 0),
    (3, 0), (1, 3), (3, 1), (0, 2),
)
BPQ = len(OFFSETS) // NQ
SCHEDULE = (
    "D0", "S0", "D1", "W0", "D2", "D3", "C0", "S1", "R0", "B0",
    "S2", "C1", "A0", "R1", "B1", "S3", "F0", "C2", "A1", "R2",
    "G0", "B2", "O0", "F1", "C3", "A2", "R3", "B3", "G1", "O1",
    "F2", "A3", "G2", "O2", "F3", "K0", "G3", "O3", "K1", "K2",
    "K3",
)


def dot(a, b):
    return jnp.dot(a, b, preferred_element_type=F32)


def dot_nt(a, b):
    return lax.dot_general(a, b, (((1,), (1,)), ((), ())), preferred_element_type=F32)


def dot_tn(a, b):
    return lax.dot_general(a, b, (((0,), (0,)), ((), ())), preferred_element_type=F32)


def layer_kernel(
    tok, cot, routes, probs, wgu_hbm, wd_hbm,
    lay_out, gtok_out, dp_out, rows_hbm, act_hbm,
    xb, tb, selp, selq, sb, xr, stg, wgu, wd, pa, cr, own, dep, s2, sn, sd, m1, m2, ga,
    oacc, ob, rr, lacc, dacc, fb, fr,
    w_sem, s1_s, s1_r, s2_s, s2_r, loc, ce_s, ce_r, m1_s, m1_r, n_s, n_r, m2_s, m2_r, ag_s, ag_r,
    rt_s, rt_r, fx_s, fx_r, hb,
):
    er = lax.axis_index("erow")
    ec = lax.axis_index("ecol")
    x, k = er // NK, er % NK
    z, y = ec // NY, ec % NY
    wdt = wd.shape[1]
    fs = wgu.shape[2] // 2
    half = xr.shape[1] * BPQ // 2
    rows = xr.shape[1] * BPQ

    def row_at(dx, dk):
        return {"erow": ((x + dx) % NX) * NK + (k + dk) % NK}

    def col_at(dz, dy):
        return {"ecol": ((z + dz) % NZ) * NY + (y + dy) % NY}

    def remote(src, dst, ss, rs, dev):
        return pltpu.make_async_remote_copy(
            src_ref=src, dst_ref=dst, send_sem=ss, recv_sem=rs, device_id=dev, device_id_type=MESH
        )

    wd_copy = pltpu.make_async_copy(wd_hbm.at[0], wd, w_sem.at[16])

    def w_copy(c):
        return pltpu.make_async_copy(
            wgu_hbm.at[0, :, :, pl.ds(pl.multiple_of(c * 128, 128), 128)], stg.at[c], w_sem.at[c]
        )

    for c in range(16):
        w_copy(c).start()
    wd_copy.start()

    bar = pltpu.get_barrier_semaphore()
    for d in range(1, NR):
        pl.semaphore_signal(bar, inc=1, device_id=row_at(d // NK, d % NK), device_id_type=MESH)
    for dz, dy in OFFSETS[1:]:
        pl.semaphore_signal(bar, inc=1, device_id=col_at(dz, dy), device_id_type=MESH)

    lane = lax.broadcasted_iota(jnp.int32, (8, 128), 1)
    row8 = lax.broadcasted_iota(jnp.int32, (8, 128), 0)
    expert = (lane % (NE * CAP)) // CAP
    member = jnp.zeros((8, 128), F32)
    weight = jnp.zeros((8, 128), F32)
    eye = jnp.where(
        lax.broadcasted_iota(jnp.int32, (8, 8), 0) == lax.broadcasted_iota(jnp.int32, (8, 8), 1), 1.0, 0.0
    ).astype(BF)
    rt = dot_nt(eye, routes[...].astype(F32).astype(BF))
    gp = dot_nt(eye, probs[...])
    for j in range(rt.shape[1]):
        hit = rt[:, j : j + 1] == expert.astype(F32)
        member = member + jnp.where(hit, 1.0, 0.0)
        weight = weight + jnp.where(hit, gp[:, j : j + 1], 0.0)
    prior = jnp.zeros((8, 128), F32)
    for t in range(7):
        prior = prior + jnp.where(row8 > t, member[t : t + 1, :], 0.0)
    place = jnp.where(prior == (lane % CAP).astype(F32), member, 0.0)
    meta = jnp.where(lane < NE * CAP, place, place * weight).astype(BF)

    def block_of(ref, r):
        return ref[:, pl.ds(pl.multiple_of(r * wdt, 128), wdt)]

    for d in range(NR):
        dst = xb if d else tb
        r = ((x + d // NK) % NX) * NK + (k + d % NK) % NK
        dst[d, :, 0:wdt] = block_of(tok, r)
        dst[d, :, wdt : 2 * wdt] = block_of(cot, r)
        dst[d, :, 2 * wdt :] = meta

    pl.semaphore_wait(bar, NR - 1 + NE - 1)

    first = []
    for d in range(1, NR):
        cp = remote(xb.at[d], tb.at[d], s1_s.at[d], s1_r.at[d], row_at(d // NK, d % NK))
        cp.start()
        first.append(cp)

    pi = lax.broadcasted_iota(jnp.int32, (256, 256), 0)
    pj = lax.broadcasted_iota(jnp.int32, (256, 256), 1)
    perm = jnp.where(pj == jnp.where(pi < 128, 2 * pi, 2 * pi - 255), 1.0, 0.0).astype(BF)

    def spread(c, carry):
        w_copy(c).wait()
        raw = stg.at[c].reshape(2 * wdt, 128)
        s, h = c // 2, c % 2
        for b in range(wdt // 128):
            v = dot(perm, raw[pl.ds(b * 256, 256), :]).astype(BF)
            wgu[s, b * 128 : (b + 1) * 128, pl.ds(pl.multiple_of(h * 128, 128), 128)] = v[:128]
            wgu[s, b * 128 : (b + 1) * 128, pl.ds(pl.multiple_of(fs + h * 128, 128), 128)] = v[128:]
        return carry

    lax.fori_loop(0, 6, spread, 0)

    for cp in first:
        cp.wait_recv()

    def sender(d):
        return ((x + NX - d // NK) % NX) * NK + (k + d) % NK

    t_all = tb[...].reshape(NR * 8, 2 * wdt + 128)
    x_all = t_all[:, 0:wdt]
    c_all = t_all[:, wdt : 2 * wdt]
    m_all = t_all[:, 2 * wdt :]
    si = lax.broadcasted_iota(jnp.int32, (rows, 128), 0)
    mi = lax.broadcasted_iota(jnp.int32, (rows, 128), 1)
    second = {}

    def stage_d(q):
        want = jnp.zeros((rows, 128), jnp.int32)
        for b in range(BPQ):
            dz, dy = OFFSETS[q * BPQ + b]
            e = ((z + dz) % NZ) * NY + (y + dy) % NY
            want = jnp.where(si // 32 == b, e, want)
        match = ((mi % (NE * CAP)) // CAP == want) & (mi % CAP == si % CAP)
        e_hot = jnp.where(match & (mi < NE * CAP), 1.0, 0.0).astype(BF)
        e_wgt = jnp.where(match & (mi >= NE * CAP), 1.0, 0.0).astype(BF)
        ti = lax.broadcasted_iota(jnp.int32, (rows, NR * 8), 1)
        sj = lax.broadcasted_iota(jnp.int32, (rows, NR * 8), 0)
        mine = (sj % 32) // CAP == sender(ti // 8)
        hot_t = jnp.where(mine, dot_nt(e_hot, m_all), 0.0).astype(BF)
        wgt_t = jnp.where(mine, dot_nt(e_wgt, m_all), 0.0).astype(BF)
        ti2 = lax.broadcasted_iota(jnp.int32, (NR * 8, rows), 0)
        sj2 = lax.broadcasted_iota(jnp.int32, (NR * 8, rows), 1)
        mine2 = (sj2 % 32) // CAP == sender(ti2 // 8)
        selq[q] = jnp.where(mine2, dot_nt(m_all, e_hot), 0.0).astype(BF)
        selp[q] = jnp.where(mine2, dot_nt(m_all, e_wgt), 0.0).astype(BF)
        xs = dot(hot_t, x_all).astype(BF).reshape(BPQ, 32, wdt)
        cs = dot(wgt_t, c_all).astype(BF).reshape(BPQ, 32, wdt)
        sb[q * BPQ : (q + 1) * BPQ, :, 0:wdt] = xs
        sb[q * BPQ : (q + 1) * BPQ, :, wdt:] = cs

    def stage_s(q):
        for i in range(q * BPQ, (q + 1) * BPQ):
            if i == 0:
                cp = pltpu.make_async_copy(sb.at[0], xr.at[0], loc.at[0])
            else:
                cp = remote(sb.at[i], xr.at[i], s2_s.at[i], s2_r.at[i], col_at(*OFFSETS[i]))
            cp.start()
            second[i] = cp

    def stage_w(half_of):
        if half_of == 0:
            lax.fori_loop(6, 16, spread, 0)
            wd_copy.wait()

    def slice_at(dx, dk):
        return ((x + dx) % NX) * NK + (k + dk) % NK

    def chunk(ref, q, lo, hi):
        return ref[q * BPQ : (q + 1) * BPQ, :, lo:hi].reshape(rows, hi - lo)

    copies = {}
    flying = []

    def send(name, *args):
        cp = remote(*args)
        cp.start()
        copies[name] = cp
        flying.append(cp)

    def partials(q, s):
        pre = dot(chunk(xr, q, 0, wdt), wgu[s])
        hg = dot_nt(chunk(xr, q, wdt, 2 * wdt), wd[pl.ds(pl.multiple_of(s * fs, fs), fs), :])
        return pre, hg

    def partial_to_partner(q, j, dx):
        pre, hg = partials(q, slice_at(dx, 1))
        pa[q, j, :, 0 : 2 * fs] = pre.astype(BF)
        pa[q, j, :, 2 * fs :] = hg.astype(BF)
        send(("ce", q, j), pa.at[q, j], cr.at[q, j], ce_s.at[q, j], ce_r.at[q, j], row_at(0, 1))

    def partial_sum(q, j, dx):
        pre, hg = partials(q, slice_at(dx, 0))
        copies["ce", q, j].wait_recv()
        return jnp.concatenate([pre, hg], axis=1) + cr[q, j].astype(F32)

    def stage_c(q):
        for i in range(q * BPQ, (q + 1) * BPQ):
            if i == 0:
                second[i].wait()
            else:
                second[i].wait_recv()
        for j, dx in enumerate((2, 1, 3)):
            partial_to_partner(q, j, dx)
        r2 = partial_sum(q, 0, 2)
        s2[q, 0] = r2[0:half].astype(BF)
        send(("m1", q, 0), s2.at[q, 0], m1.at[q, 0], m1_s.at[q, 0], m1_r.at[q, 0], row_at(1, 0))
        s2[q, 1] = r2[half:rows].astype(BF)
        send(("m1", q, 1), s2.at[q, 1], m1.at[q, 1], m1_s.at[q, 1], m1_r.at[q, 1], row_at(3, 0))
        r1 = partial_sum(q, 1, 1)
        sn[q, 0] = r1[half:rows].astype(BF)
        send(("n", q, 0), sn.at[q, 0], m2.at[q, 0, 1], n_s.at[q, 0], n_r.at[q, 0], row_at(1, 0))
        dep[q, 0] = r1[0:half]
        r3 = partial_sum(q, 2, 3)
        sn[q, 1] = r3[0:half].astype(BF)
        send(("n", q, 1), sn.at[q, 1], m2.at[q, 1, 0], n_s.at[q, 1], n_r.at[q, 1], row_at(3, 0))
        dep[q, 1] = r3[half:rows]

    def stage_b(q):
        partial_to_partner(q, 3, 0)
        own[q] = partial_sum(q, 3, 0)

    def stage_r(q):
        copies["m1", q, 0].wait_recv()
        sd[q, 0] = (dep[q, 0] + m1[q, 0].astype(F32)).astype(BF)
        send(("m2", q, 0), sd.at[q, 0], m2.at[q, 0, 0], m2_s.at[q, 0], m2_r.at[q, 0], row_at(1, 0))
        copies["m1", q, 1].wait_recv()
        sd[q, 1] = (dep[q, 1] + m1[q, 1].astype(F32)).astype(BF)
        send(("m2", q, 1), sd.at[q, 1], m2.at[q, 1, 1], m2_s.at[q, 1], m2_r.at[q, 1], row_at(3, 0))

    def stage_a(q):
        for d in range(2):
            copies["n", q, d].wait_recv()
            copies["m2", q, d].wait_recv()
        for h in range(2):
            lo, hi = h * half, (h + 1) * half
            tot = own[q, lo:hi, :] + m2[q, 0, h].astype(F32) + m2[q, 1, h].astype(F32)
            g, u, hg = tot[:, 0:fs], tot[:, fs : 2 * fs], tot[:, 2 * fs :]
            s = 1.0 / (1.0 + jnp.exp(-g))
            a = g * s
            ga[q, 0, lo:hi, 0:fs] = (a * u).astype(BF)
            ga[q, 0, lo:hi, fs : 2 * fs] = (hg * u * s * (1.0 + g * (1.0 - s))).astype(BF)
            ga[q, 0, lo:hi, 2 * fs :] = (hg * a).astype(BF)
        src = ga.at[q, 0]
        send(("ag", q, 0), src, ga.at[q, 2], ag_s.at[q, 0], ag_r.at[q, 0], row_at(1, 0))
        send(("ag", q, 1), src, ga.at[q, 6], ag_s.at[q, 1], ag_r.at[q, 1], row_at(3, 0))
        send(("ag", q, 2), src, ga.at[q, 1], ag_s.at[q, 2], ag_r.at[q, 2], row_at(0, 1))

    def stage_f(q):
        copies["ag", q, 0].wait_recv()
        send(("ag", q, 3), ga.at[q, 2, 0:half], ga.at[q, 4, 0:half], ag_s.at[q, 3], ag_r.at[q, 3], row_at(1, 0))
        send(("ag", q, 4), ga.at[q, 2], ga.at[q, 3], ag_s.at[q, 4], ag_r.at[q, 4], row_at(0, 1))
        copies["ag", q, 1].wait_recv()
        send(
            ("ag", q, 5), ga.at[q, 6, half:rows], ga.at[q, 4, half:rows], ag_s.at[q, 5], ag_r.at[q, 5], row_at(3, 0)
        )
        send(("ag", q, 6), ga.at[q, 6], ga.at[q, 7], ag_s.at[q, 6], ag_r.at[q, 6], row_at(0, 1))

    def stage_g(q):
        copies["ag", q, 3].wait_recv()
        copies["ag", q, 5].wait_recv()
        send(("ag", q, 7), ga.at[q, 4], ga.at[q, 5], ag_s.at[q, 7], ag_r.at[q, 7], row_at(0, 1))

    stores = []

    def stage_o(q):
        for j in (2, 4, 6, 7):
            copies["ag", q, j].wait_recv()
        for j in range(NR):
            s = slice_at(NX - j // NK, j % NK)
            cp = pltpu.make_async_copy(ga.at[q, j], act_hbm.at[s, pl.ds(q * rows, rows)], hb.at[q * NR + j])
            cp.start()
            stores.append(cp)

        def term(dx):
            s0, s1 = slice_at(NX - dx, 0), slice_at(NX - dx, 1)
            p0, p1 = ga[q, 2 * dx], ga[q, 2 * dx + 1]
            w0 = wd[pl.ds(pl.multiple_of(s0 * fs, fs), fs), :]
            w1 = wd[pl.ds(pl.multiple_of(s1 * fs, fs), fs), :]
            out = dot(p0[:, 0:fs], w0) + dot(p1[:, 0:fs], w1)
            grad = dot_nt(p0[:, fs:], wgu[s0]) + dot_nt(p1[:, fs:], wgu[s1])
            return out, grad

        out, grad = term(0)
        oacc[:, 0:wdt] = out
        oacc[:, wdt:] = grad

        def more(dx, carry):
            out, grad = term(dx)
            oacc[:, 0:wdt] += out
            oacc[:, wdt:] += grad
            return carry

        lax.fori_loop(1, NX, more, 0)
        ob[q * BPQ : (q + 1) * BPQ] = oacc[...].astype(BF).reshape(BPQ, 32, 2 * wdt)
        for i in range(q * BPQ, (q + 1) * BPQ):
            if i == 0:
                cp = pltpu.make_async_copy(ob.at[0], rr.at[0], loc.at[1])
                cp.start()
                copies["rt", 0] = cp
            else:
                dz, dy = OFFSETS[i]
                send(("rt", i), ob.at[i], rr.at[i], rt_s.at[i], rt_r.at[i], col_at(NZ - dz, NY - dy))

    def stage_k(q):
        for i in range(q * BPQ, (q + 1) * BPQ):
            if i == 0:
                copies["rt", 0].wait()
            else:
                copies["rt", i].wait_recv()
        eo = chunk(rr, q, 0, wdt)
        gr = chunk(rr, q, wdt, 2 * wdt)
        hot = selq[q]
        lay = dot(selp[q], eo)
        gt = dot(hot, gr)
        dots = dot_nt(tb[...].reshape(NR * 8, 2 * wdt + 128)[:, wdt : 2 * wdt], eo) * hot.astype(F32)
        li = lax.broadcasted_iota(jnp.int32, (NR * 8, 128), 1)
        dp = jnp.zeros((NR * 8, 128), F32)
        for b in range(BPQ):
            dz, dy = OFFSETS[q * BPQ + b]
            e = ((z + dz) % NZ) * NY + (y + dy) % NY
            total = jnp.sum(jnp.where(li // 32 == b, dots, 0.0), axis=1, keepdims=True)
            dp = dp + jnp.where(li == e, total, 0.0)
        if q == 0:
            lacc[:, 0:wdt] = lay
            lacc[:, wdt:] = gt
            dacc[...] = dp
        else:
            lacc[:, 0:wdt] += lay
            lacc[:, wdt:] += gt
            dacc[...] += dp

    stages = {"D": stage_d, "S": stage_s, "W": stage_w, "C": stage_c, "B": stage_b, "R": stage_r, "A": stage_a, "F": stage_f, "G": stage_g, "O": stage_o, "K": stage_k}
    for step in SCHEDULE:
        stages[step[0]](int(step[1:]))
        if step == "C3":
            cp = pltpu.make_async_copy(xr, rows_hbm, hb.at[NQ * NR])
            cp.start()
            stores.append(cp)

    for d in range(NR):
        dst = fb if d else fr
        dst[d, :, 0 : 2 * wdt] = lacc[d * 8 : (d + 1) * 8, :].astype(BF)
        dst[d, :, 2 * wdt :] = dacc[d * 8 : (d + 1) * 8, :].astype(BF)
    last = []
    for d in range(1, NR):
        cp = remote(fb.at[d], fr.at[d], fx_s.at[d], fx_r.at[d], row_at(NX - d // NK, d % NK))
        cp.start()
        last.append(cp)

    for cp in first:
        cp.wait_send()
    for i in range(1, NE):
        second[i].wait_send()
    for cp in flying:
        cp.wait_send()
    for cp in stores:
        cp.wait()

    total = jnp.zeros((8, 128), F32)
    for d in range(NR):
        if d:
            last[d - 1].wait_recv()
        r = slice_at(d // NK, d % NK)
        cols = pl.ds(pl.multiple_of(r * wdt, 128), wdt)
        lay_out[:, cols] = fr[d, :, 0:wdt]
        gtok_out[:, cols] = fr[d, :, wdt : 2 * wdt]
        total = total + fr[d, :, 2 * wdt :].astype(F32)
    picked = jnp.zeros((8, 128), F32)
    for j in range(rt.shape[1]):
        val = jnp.sum(jnp.where(rt[:, j : j + 1] == lane.astype(F32), total, 0.0), axis=1, keepdims=True)
        picked = picked + jnp.where(lane == j, val, 0.0)
    dp_out[...] = picked.T[0 : rt.shape[1], :]
    for cp in last:
        cp.wait_send()


def layer(tokens, cotangent, routes, gate_probs, w_gate_up, w_down):
    width = w_gate_up.shape[1]
    hid = w_gate_up.shape[3]
    fs = hid // NR
    tok = tokens.shape[0]
    blk = NR * CAP
    rows = BPQ * blk
    vm = pltpu.VMEM
    dma = pltpu.SemaphoreType.DMA
    scratch = [
        vm((NR, tok, 2 * width + 128), BF),
        vm((NR, tok, 2 * width + 128), BF),
        vm((NQ, NR * tok, rows), BF),
        vm((NQ, NR * tok, rows), BF),
        vm((NE, blk, 2 * width), BF),
        vm((NE, blk, 2 * width), BF),
        vm((hid // 128, width, 2, 128), BF),
        vm((NR, width, 2 * fs), BF),
        vm((hid, width), BF),
        vm((NQ, NX, rows, 3 * fs), BF),
        vm((NQ, NX, rows, 3 * fs), BF),
        vm((NQ, rows, 3 * fs), F32),
        vm((NQ, 2, rows // 2, 3 * fs), F32),
        vm((NQ, 2, rows // 2, 3 * fs), BF),
        vm((NQ, 2, rows // 2, 3 * fs), BF),
        vm((NQ, 2, rows // 2, 3 * fs), BF),
        vm((NQ, 2, rows // 2, 3 * fs), BF),
        vm((NQ, 2, 2, rows // 2, 3 * fs), BF),
        vm((NQ, NR, rows, 3 * fs), BF),
        vm((rows, 2 * width), F32),
        vm((NE, blk, 2 * width), BF),
        vm((NE, blk, 2 * width), BF),
        vm((NR * tok, 2 * width), F32),
        vm((NR * tok, 128), F32),
        vm((NR, tok, 2 * width + 128), BF),
        vm((NR, tok, 2 * width + 128), BF),
        dma((17,)),
        dma((NR,)), dma((NR,)),
        dma((NE,)), dma((NE,)),
        dma((2,)),
        dma((NQ, NX)), dma((NQ, NX)),
        dma((NQ, 2)), dma((NQ, 2)),
        dma((NQ, 2)), dma((NQ, 2)),
        dma((NQ, 2)), dma((NQ, 2)),
        dma((NQ, NR)), dma((NQ, NR)),
        dma((NE,)), dma((NE,)),
        dma((NR,)), dma((NR,)),
        dma((NQ * NR + 1,)),
    ]
    vmem = pl.BlockSpec(memory_space=pltpu.VMEM)
    hbm = pl.BlockSpec(memory_space=pl.ANY)
    return pl.pallas_call(
        layer_kernel,
        name="layer",
        out_shape=(
            jax.ShapeDtypeStruct(tokens.shape, BF),
            jax.ShapeDtypeStruct(tokens.shape, BF),
            jax.ShapeDtypeStruct(routes.shape, F32),
            jax.ShapeDtypeStruct((NE, blk, 2 * width), BF),
            jax.ShapeDtypeStruct((NR, NQ * rows, 3 * fs), BF),
        ),
        in_specs=[vmem, vmem, vmem, vmem, hbm, hbm],
        out_specs=(vmem, vmem, vmem, hbm, hbm),
        scratch_shapes=scratch,
        compiler_params=pltpu.CompilerParams(
            collective_id=0, has_side_effects=True, vmem_limit_bytes=60 << 20
        ),
    )(tokens, cotangent, routes, gate_probs, w_gate_up, w_down)


def grads_kernel(rows_ref, act_ref, a_ref, b_ref, c_ref, gd_ref, ggu_hbm, a_out, b_out, c_out, xt, stg, sem):
    s = pl.program_id(0)
    slot = s % 2
    width = rows_ref.shape[1] // 2
    fs = gd_ref.shape[1]

    def out_copy(step, h):
        c = step * 2 + h
        return pltpu.make_async_copy(
            stg.at[step % 2, h],
            ggu_hbm.at[0, :, :, pl.ds(pl.multiple_of(c * 128, 128), 128)],
            sem.at[step % 2, h],
        )

    @pl.when(s >= 2)
    def _():
        for h in range(2):
            out_copy(s - 2, h).wait()

    @pl.when(s == 0)
    def _():
        a_out[...] = a_ref[...]
        b_out[...] = b_ref[...]
        c_out[...] = c_ref[...]
        xt[...] = rows_ref[:, 0:width].T

    act = act_ref[0]
    gd_ref[0] = dot_tn(act[:, 0:fs], rows_ref[:, width:]).astype(BF)
    pi = lax.broadcasted_iota(jnp.int32, (256, 256), 0)
    pj = lax.broadcasted_iota(jnp.int32, (256, 256), 1)
    perm = jnp.where(pi == jnp.where(pj < 128, 2 * pj, 2 * pj - 255), 1.0, 0.0).astype(BF)
    g = dot(xt[...], act[:, fs:]).astype(BF)
    for b in range(width // 128):
        gb = g[b * 128 : (b + 1) * 128]
        v = dot(perm, jnp.concatenate([gb[:, 0:fs], gb[:, fs:]], axis=0)).astype(BF)
        for h in range(2):
            stg.at[slot, h].reshape(2 * width, 128)[pl.ds(b * 256, 256), :] = v[:, h * 128 : (h + 1) * 128]
    for h in range(2):
        out_copy(s, h).start()

    @pl.when(s == pl.num_programs(0) - 1)
    def _():
        for h in range(2):
            out_copy(s - 1, h).wait()
        for h in range(2):
            out_copy(s, h).wait()


def weight_grads(rows, act, small, width, hid):
    fs = hid // NR
    n = rows.shape[0]
    return pl.pallas_call(
        grads_kernel,
        name="weight_grads",
        grid=(NR,),
        out_shape=(
            jax.ShapeDtypeStruct((1, hid, width), BF),
            jax.ShapeDtypeStruct((1, width, 2, hid), BF),
            *(jax.ShapeDtypeStruct(v.shape, v.dtype) for v in small),
        ),
        in_specs=[
            pl.BlockSpec((n, 2 * width), lambda s: (0, 0)),
            pl.BlockSpec((1, n, 3 * fs), lambda s: (s, 0, 0)),
            *(pl.BlockSpec(v.shape, lambda s: (0, 0)) for v in small),
        ],
        out_specs=(
            pl.BlockSpec((1, fs, width), lambda s: (0, s, 0)),
            pl.BlockSpec(memory_space=pl.ANY),
            *(pl.BlockSpec(v.shape, lambda s: (0, 0)) for v in small),
        ),
        scratch_shapes=[
            pltpu.VMEM((width, n), BF),
            pltpu.VMEM((2, 2, width, 2, 128), BF),
            pltpu.SemaphoreType.DMA((2, 2)),
        ],
        compiler_params=pltpu.CompilerParams(vmem_limit_bytes=60 << 20),
    )(rows, act, *small)


def on_device(tokens, routes, gate_probs, cotangent, w_gate_up, w_down):
    width, hid = w_gate_up.shape[1], w_gate_up.shape[3]
    layer_out, grad_tokens, dprob, rows, act = layer(
        tokens, cotangent, routes.T, gate_probs.T, w_gate_up, w_down
    )
    grad_down, grad_gate_up, layer_out, grad_tokens, dprob = weight_grads(
        rows.reshape(-1, 2 * width), act, (layer_out, grad_tokens, dprob), width, hid
    )
    return (layer_out, grad_tokens, dprob.T, grad_gate_up, grad_down)


def solution(mesh):
    rows = P(("erow", "ecol"), None)
    up, down = P("ecol", "erow", None, None), P("ecol", None, "erow")
    return jax.shard_map(
        on_device,
        mesh=mesh,
        in_specs=(rows, rows, rows, rows, up, down),
        out_specs=(rows, rows, rows, up, down),
        check_vma=False,
    )
```

```python
import jax
import jax.numpy as jnp
from jax import lax
from jax.experimental import pallas as pl
from jax.experimental.pallas import tpu as pltpu
from jax.sharding import PartitionSpec as P

BF = jnp.bfloat16
F32 = jnp.float32
MESH = pl.DeviceIdType.MESH
NX, NK, NZ, NY = 4, 2, 4, 4
NR, NE = NX * NK, NZ * NY
CAP = 4
NQ = 4
OFFSETS = (
    (0, 0), (0, 1), (0, 3), (1, 0),
    (2, 2), (1, 2), (2, 1), (1, 1),
    (3, 2), (2, 3), (3, 3), (2, 0),
    (3, 0), (1, 3), (3, 1), (0, 2),
)
BPQ = len(OFFSETS) // NQ
SCHEDULE = (
    "D0", "S0", "D2", "D1", "S1", "W0", "C0", "B0", "R0", "S2",
    "C1", "D3", "S3", "A0", "R1", "F0", "C2", "B1", "A1", "G0",
    "O0", "R2", "B2", "F1", "C3", "A2", "R3", "B3", "G1", "O1",
    "F2", "A3", "K0", "G2", "O2", "F3", "G3", "O3", "K1", "K2",
    "K3",
)


def dot(a, b):
    return jnp.dot(a, b, preferred_element_type=F32)


def dot_nt(a, b):
    return lax.dot_general(a, b, (((1,), (1,)), ((), ())), preferred_element_type=F32)


def dot_tn(a, b):
    return lax.dot_general(a, b, (((0,), (0,)), ((), ())), preferred_element_type=F32)


def layer_kernel(
    tok, cot, routes, probs, wgu_hbm, wd_hbm,
    lay_out, gtok_out, dp_out, rows_hbm, act_hbm,
    xb, tb, selp, selq, sb, xr, stg, wgu, wd, pa, cr, own, dep, s2, sn, sd, m1, m2, ga,
    oacc, ob, rr, lacc, dacc, fb, fr,
    w_sem, s1_s, s1_r, s2_s, s2_r, loc, ce_s, ce_r, m1_s, m1_r, n_s, n_r, m2_s, m2_r, ag_s, ag_r,
    rt_s, rt_r, fx_s, fx_r, hb,
):
    er = lax.axis_index("erow")
    ec = lax.axis_index("ecol")
    x, k = er // NK, er % NK
    z, y = ec // NY, ec % NY
    wdt = wd.shape[1]
    fs = wgu.shape[2] // 2
    half = xr.shape[1] * BPQ // 2
    rows = xr.shape[1] * BPQ

    def row_at(dx, dk):
        return {"erow": ((x + dx) % NX) * NK + (k + dk) % NK}

    def col_at(dz, dy):
        return {"ecol": ((z + dz) % NZ) * NY + (y + dy) % NY}

    def remote(src, dst, ss, rs, dev):
        return pltpu.make_async_remote_copy(
            src_ref=src, dst_ref=dst, send_sem=ss, recv_sem=rs, device_id=dev, device_id_type=MESH
        )

    wd_copy = pltpu.make_async_copy(wd_hbm.at[0], wd, w_sem.at[16])

    def w_copy(c):
        return pltpu.make_async_copy(
            wgu_hbm.at[0, :, :, pl.ds(pl.multiple_of(c * 128, 128), 128)], stg.at[c], w_sem.at[c]
        )

    for c in range(16):
        w_copy(c).start()
    wd_copy.start()

    bar = pltpu.get_barrier_semaphore()
    for d in range(1, NR):
        pl.semaphore_signal(bar, inc=1, device_id=row_at(d // NK, d % NK), device_id_type=MESH)
    for dz, dy in OFFSETS[1:]:
        pl.semaphore_signal(bar, inc=1, device_id=col_at(dz, dy), device_id_type=MESH)

    lane = lax.broadcasted_iota(jnp.int32, (8, 128), 1)
    row8 = lax.broadcasted_iota(jnp.int32, (8, 128), 0)
    expert = (lane % (NE * CAP)) // CAP
    member = jnp.zeros((8, 128), F32)
    weight = jnp.zeros((8, 128), F32)
    eye = jnp.where(
        lax.broadcasted_iota(jnp.int32, (8, 8), 0) == lax.broadcasted_iota(jnp.int32, (8, 8), 1), 1.0, 0.0
    ).astype(BF)
    rt = dot_nt(eye, routes[...].astype(F32).astype(BF))
    gp = dot_nt(eye, probs[...])
    for j in range(rt.shape[1]):
        hit = rt[:, j : j + 1] == expert.astype(F32)
        member = member + jnp.where(hit, 1.0, 0.0)
        weight = weight + jnp.where(hit, gp[:, j : j + 1], 0.0)
    prior = jnp.zeros((8, 128), F32)
    for t in range(7):
        prior = prior + jnp.where(row8 > t, member[t : t + 1, :], 0.0)
    place = jnp.where(prior == (lane % CAP).astype(F32), member, 0.0)
    meta = jnp.where(lane < NE * CAP, place, place * weight).astype(BF)

    def block_of(ref, r):
        return ref[:, pl.ds(pl.multiple_of(r * wdt, 128), wdt)]

    for d in range(NR):
        dst = xb if d else tb
        r = ((x + d // NK) % NX) * NK + (k + d % NK) % NK
        dst[d, :, 0:wdt] = block_of(tok, r)
        dst[d, :, wdt : 2 * wdt] = block_of(cot, r)
        dst[d, :, 2 * wdt :] = meta

    pl.semaphore_wait(bar, NR - 1 + NE - 1)

    first = []
    for d in range(1, NR):
        cp = remote(xb.at[d], tb.at[d], s1_s.at[d], s1_r.at[d], row_at(d // NK, d % NK))
        cp.start()
        first.append(cp)

    pi = lax.broadcasted_iota(jnp.int32, (256, 256), 0)
    pj = lax.broadcasted_iota(jnp.int32, (256, 256), 1)
    perm = jnp.where(pj == jnp.where(pi < 128, 2 * pi, 2 * pi - 255), 1.0, 0.0).astype(BF)

    def spread(c, carry):
        w_copy(c).wait()
        raw = stg.at[c].reshape(2 * wdt, 128)
        s, h = c // 2, c % 2
        for b in range(wdt // 128):
            v = dot(perm, raw[pl.ds(b * 256, 256), :]).astype(BF)
            wgu[s, b * 128 : (b + 1) * 128, pl.ds(pl.multiple_of(h * 128, 128), 128)] = v[:128]
            wgu[s, b * 128 : (b + 1) * 128, pl.ds(pl.multiple_of(fs + h * 128, 128), 128)] = v[128:]
        return carry

    lax.fori_loop(0, 6, spread, 0)

    for cp in first:
        cp.wait_recv()

    def sender(d):
        return ((x + NX - d // NK) % NX) * NK + (k + d) % NK

    t_all = tb[...].reshape(NR * 8, 2 * wdt + 128)
    x_all = t_all[:, 0:wdt]
    c_all = t_all[:, wdt : 2 * wdt]
    m_all = t_all[:, 2 * wdt :]
    si = lax.broadcasted_iota(jnp.int32, (rows, 128), 0)
    mi = lax.broadcasted_iota(jnp.int32, (rows, 128), 1)
    second = {}

    def stage_d(q):
        want = jnp.zeros((rows, 128), jnp.int32)
        for b in range(BPQ):
            dz, dy = OFFSETS[q * BPQ + b]
            e = ((z + dz) % NZ) * NY + (y + dy) % NY
            want = jnp.where(si // 32 == b, e, want)
        match = ((mi % (NE * CAP)) // CAP == want) & (mi % CAP == si % CAP)
        e_hot = jnp.where(match & (mi < NE * CAP), 1.0, 0.0).astype(BF)
        e_wgt = jnp.where(match & (mi >= NE * CAP), 1.0, 0.0).astype(BF)
        ti = lax.broadcasted_iota(jnp.int32, (rows, NR * 8), 1)
        sj = lax.broadcasted_iota(jnp.int32, (rows, NR * 8), 0)
        mine = (sj % 32) // CAP == sender(ti // 8)
        hot_t = jnp.where(mine, dot_nt(e_hot, m_all), 0.0).astype(BF)
        wgt_t = jnp.where(mine, dot_nt(e_wgt, m_all), 0.0).astype(BF)
        ti2 = lax.broadcasted_iota(jnp.int32, (NR * 8, rows), 0)
        sj2 = lax.broadcasted_iota(jnp.int32, (NR * 8, rows), 1)
        mine2 = (sj2 % 32) // CAP == sender(ti2 // 8)
        selq[q] = jnp.where(mine2, dot_nt(m_all, e_hot), 0.0).astype(BF)
        selp[q] = jnp.where(mine2, dot_nt(m_all, e_wgt), 0.0).astype(BF)
        xs = dot(hot_t, x_all).astype(BF).reshape(BPQ, 32, wdt)
        cs = dot(wgt_t, c_all).astype(BF).reshape(BPQ, 32, wdt)
        sb[q * BPQ : (q + 1) * BPQ, :, 0:wdt] = xs
        sb[q * BPQ : (q + 1) * BPQ, :, wdt:] = cs

    def stage_s(q):
        for i in range(q * BPQ, (q + 1) * BPQ):
            if i == 0:
                cp = pltpu.make_async_copy(sb.at[0], xr.at[0], loc.at[0])
            else:
                cp = remote(sb.at[i], xr.at[i], s2_s.at[i], s2_r.at[i], col_at(*OFFSETS[i]))
            cp.start()
            second[i] = cp

    def stage_w(half_of):
        if half_of == 0:
            lax.fori_loop(6, 16, spread, 0)
            wd_copy.wait()

    def slice_at(dx, dk):
        return ((x + dx) % NX) * NK + (k + dk) % NK

    def chunk(ref, q, lo, hi):
        return ref[q * BPQ : (q + 1) * BPQ, :, lo:hi].reshape(rows, hi - lo)

    copies = {}
    flying = []

    def send(name, *args):
        cp = remote(*args)
        cp.start()
        copies[name] = cp
        flying.append(cp)

    def partials(q, s):
        pre = dot(chunk(xr, q, 0, wdt), wgu[s])
        hg = dot_nt(chunk(xr, q, wdt, 2 * wdt), wd[pl.ds(pl.multiple_of(s * fs, fs), fs), :])
        return pre, hg

    def partial_to_partner(q, j, dx):
        pre, hg = partials(q, slice_at(dx, 1))
        pa[q, j, :, 0 : 2 * fs] = pre.astype(BF)
        pa[q, j, :, 2 * fs :] = hg.astype(BF)
        send(("ce", q, j), pa.at[q, j], cr.at[q, j], ce_s.at[q, j], ce_r.at[q, j], row_at(0, 1))

    def partial_sum(q, j, dx):
        pre, hg = partials(q, slice_at(dx, 0))
        copies["ce", q, j].wait_recv()
        return jnp.concatenate([pre, hg], axis=1) + cr[q, j].astype(F32)

    def stage_c(q):
        for i in range(q * BPQ, (q + 1) * BPQ):
            if i == 0:
                second[i].wait()
            else:
                second[i].wait_recv()
        for j, dx in enumerate((2, 1, 3)):
            partial_to_partner(q, j, dx)
        r2 = partial_sum(q, 0, 2)
        s2[q, 0] = r2[0:half].astype(BF)
        send(("m1", q, 0), s2.at[q, 0], m1.at[q, 0], m1_s.at[q, 0], m1_r.at[q, 0], row_at(1, 0))
        s2[q, 1] = r2[half:rows].astype(BF)
        send(("m1", q, 1), s2.at[q, 1], m1.at[q, 1], m1_s.at[q, 1], m1_r.at[q, 1], row_at(3, 0))
        r1 = partial_sum(q, 1, 1)
        sn[q, 0] = r1[half:rows].astype(BF)
        send(("n", q, 0), sn.at[q, 0], m2.at[q, 0, 1], n_s.at[q, 0], n_r.at[q, 0], row_at(1, 0))
        dep[q, 0] = r1[0:half]
        r3 = partial_sum(q, 2, 3)
        sn[q, 1] = r3[0:half].astype(BF)
        send(("n", q, 1), sn.at[q, 1], m2.at[q, 1, 0], n_s.at[q, 1], n_r.at[q, 1], row_at(3, 0))
        dep[q, 1] = r3[half:rows]

    def stage_b(q):
        partial_to_partner(q, 3, 0)
        own[q] = partial_sum(q, 3, 0)

    def stage_r(q):
        copies["m1", q, 0].wait_recv()
        sd[q, 0] = (dep[q, 0] + m1[q, 0].astype(F32)).astype(BF)
        send(("m2", q, 0), sd.at[q, 0], m2.at[q, 0, 0], m2_s.at[q, 0], m2_r.at[q, 0], row_at(1, 0))
        copies["m1", q, 1].wait_recv()
        sd[q, 1] = (dep[q, 1] + m1[q, 1].astype(F32)).astype(BF)
        send(("m2", q, 1), sd.at[q, 1], m2.at[q, 1, 1], m2_s.at[q, 1], m2_r.at[q, 1], row_at(3, 0))

    def stage_a(q):
        for d in range(2):
            copies["n", q, d].wait_recv()
            copies["m2", q, d].wait_recv()
        for h in range(2):
            lo, hi = h * half, (h + 1) * half
            tot = own[q, lo:hi, :] + m2[q, 0, h].astype(F32) + m2[q, 1, h].astype(F32)
            g, u, hg = tot[:, 0:fs], tot[:, fs : 2 * fs], tot[:, 2 * fs :]
            s = 1.0 / (1.0 + jnp.exp(-g))
            a = g * s
            ga[q, 0, lo:hi, 0:fs] = (a * u).astype(BF)
            ga[q, 0, lo:hi, fs : 2 * fs] = (hg * u * s * (1.0 + g * (1.0 - s))).astype(BF)
            ga[q, 0, lo:hi, 2 * fs :] = (hg * a).astype(BF)
        src = ga.at[q, 0]
        send(("ag", q, 0), src, ga.at[q, 2], ag_s.at[q, 0], ag_r.at[q, 0], row_at(1, 0))
        send(("ag", q, 1), src, ga.at[q, 6], ag_s.at[q, 1], ag_r.at[q, 1], row_at(3, 0))
        send(("ag", q, 2), src, ga.at[q, 1], ag_s.at[q, 2], ag_r.at[q, 2], row_at(0, 1))

    def stage_f(q):
        copies["ag", q, 0].wait_recv()
        send(("ag", q, 3), ga.at[q, 2, 0:half], ga.at[q, 4, 0:half], ag_s.at[q, 3], ag_r.at[q, 3], row_at(1, 0))
        send(("ag", q, 4), ga.at[q, 2], ga.at[q, 3], ag_s.at[q, 4], ag_r.at[q, 4], row_at(0, 1))
        copies["ag", q, 1].wait_recv()
        send(
            ("ag", q, 5), ga.at[q, 6, half:rows], ga.at[q, 4, half:rows], ag_s.at[q, 5], ag_r.at[q, 5], row_at(3, 0)
        )
        send(("ag", q, 6), ga.at[q, 6], ga.at[q, 7], ag_s.at[q, 6], ag_r.at[q, 6], row_at(0, 1))

    def stage_g(q):
        copies["ag", q, 3].wait_recv()
        copies["ag", q, 5].wait_recv()
        send(("ag", q, 7), ga.at[q, 4], ga.at[q, 5], ag_s.at[q, 7], ag_r.at[q, 7], row_at(0, 1))

    stores = []

    def stage_o(q):
        for j in (2, 4, 6, 7):
            copies["ag", q, j].wait_recv()
        for j in range(NR):
            s = slice_at(NX - j // NK, j % NK)
            cp = pltpu.make_async_copy(ga.at[q, j], act_hbm.at[s, pl.ds(q * rows, rows)], hb.at[q * NR + j])
            cp.start()
            stores.append(cp)

        def term(dx):
            s0, s1 = slice_at(NX - dx, 0), slice_at(NX - dx, 1)
            p0, p1 = ga[q, 2 * dx], ga[q, 2 * dx + 1]
            w0 = wd[pl.ds(pl.multiple_of(s0 * fs, fs), fs), :]
            w1 = wd[pl.ds(pl.multiple_of(s1 * fs, fs), fs), :]
            out = dot(p0[:, 0:fs], w0) + dot(p1[:, 0:fs], w1)
            grad = dot_nt(p0[:, fs:], wgu[s0]) + dot_nt(p1[:, fs:], wgu[s1])
            return out, grad

        out, grad = term(0)
        oacc[:, 0:wdt] = out
        oacc[:, wdt:] = grad

        def more(dx, carry):
            out, grad = term(dx)
            oacc[:, 0:wdt] += out
            oacc[:, wdt:] += grad
            return carry

        lax.fori_loop(1, NX, more, 0)
        ob[q * BPQ : (q + 1) * BPQ] = oacc[...].astype(BF).reshape(BPQ, 32, 2 * wdt)
        for i in range(q * BPQ, (q + 1) * BPQ):
            if i == 0:
                cp = pltpu.make_async_copy(ob.at[0], rr.at[0], loc.at[1])
                cp.start()
                copies["rt", 0] = cp
            else:
                dz, dy = OFFSETS[i]
                send(("rt", i), ob.at[i], rr.at[i], rt_s.at[i], rt_r.at[i], col_at(NZ - dz, NY - dy))

    def stage_k(q):
        for i in range(q * BPQ, (q + 1) * BPQ):
            if i == 0:
                copies["rt", 0].wait()
            else:
                copies["rt", i].wait_recv()
        eo = chunk(rr, q, 0, wdt)
        gr = chunk(rr, q, wdt, 2 * wdt)
        hot = selq[q]
        lay = dot(selp[q], eo)
        gt = dot(hot, gr)
        dots = dot_nt(tb[...].reshape(NR * 8, 2 * wdt + 128)[:, wdt : 2 * wdt], eo) * hot.astype(F32)
        li = lax.broadcasted_iota(jnp.int32, (NR * 8, 128), 1)
        dp = jnp.zeros((NR * 8, 128), F32)
        for b in range(BPQ):
            dz, dy = OFFSETS[q * BPQ + b]
            e = ((z + dz) % NZ) * NY + (y + dy) % NY
            total = jnp.sum(jnp.where(li // 32 == b, dots, 0.0), axis=1, keepdims=True)
            dp = dp + jnp.where(li == e, total, 0.0)
        if q == 0:
            lacc[:, 0:wdt] = lay
            lacc[:, wdt:] = gt
            dacc[...] = dp
        else:
            lacc[:, 0:wdt] += lay
            lacc[:, wdt:] += gt
            dacc[...] += dp

    stages = {"D": stage_d, "S": stage_s, "W": stage_w, "C": stage_c, "B": stage_b, "R": stage_r, "A": stage_a, "F": stage_f, "G": stage_g, "O": stage_o, "K": stage_k}
    for step in SCHEDULE:
        stages[step[0]](int(step[1:]))
        if step == "C3":
            cp = pltpu.make_async_copy(xr, rows_hbm, hb.at[NQ * NR])
            cp.start()
            stores.append(cp)

    for d in range(NR):
        dst = fb if d else fr
        dst[d, :, 0 : 2 * wdt] = lacc[d * 8 : (d + 1) * 8, :].astype(BF)
        dst[d, :, 2 * wdt :] = dacc[d * 8 : (d + 1) * 8, :].astype(BF)
    last = []
    for d in range(1, NR):
        cp = remote(fb.at[d], fr.at[d], fx_s.at[d], fx_r.at[d], row_at(NX - d // NK, d % NK))
        cp.start()
        last.append(cp)

    for cp in first:
        cp.wait_send()
    for i in range(1, NE):
        second[i].wait_send()
    for cp in flying:
        cp.wait_send()
    for cp in stores:
        cp.wait()

    total = jnp.zeros((8, 128), F32)
    for d in range(NR):
        if d:
            last[d - 1].wait_recv()
        r = slice_at(d // NK, d % NK)
        cols = pl.ds(pl.multiple_of(r * wdt, 128), wdt)
        lay_out[:, cols] = fr[d, :, 0:wdt]
        gtok_out[:, cols] = fr[d, :, wdt : 2 * wdt]
        total = total + fr[d, :, 2 * wdt :].astype(F32)
    picked = jnp.zeros((8, 128), F32)
    for j in range(rt.shape[1]):
        val = jnp.sum(jnp.where(rt[:, j : j + 1] == lane.astype(F32), total, 0.0), axis=1, keepdims=True)
        picked = picked + jnp.where(lane == j, val, 0.0)
    dp_out[...] = picked.T[0 : rt.shape[1], :]
    for cp in last:
        cp.wait_send()


def layer(tokens, cotangent, routes, gate_probs, w_gate_up, w_down):
    width = w_gate_up.shape[1]
    hid = w_gate_up.shape[3]
    fs = hid // NR
    tok = tokens.shape[0]
    blk = NR * CAP
    rows = BPQ * blk
    vm = pltpu.VMEM
    dma = pltpu.SemaphoreType.DMA
    scratch = [
        vm((NR, tok, 2 * width + 128), BF),
        vm((NR, tok, 2 * width + 128), BF),
        vm((NQ, NR * tok, rows), BF),
        vm((NQ, NR * tok, rows), BF),
        vm((NE, blk, 2 * width), BF),
        vm((NE, blk, 2 * width), BF),
        vm((hid // 128, width, 2, 128), BF),
        vm((NR, width, 2 * fs), BF),
        vm((hid, width), BF),
        vm((NQ, NX, rows, 3 * fs), BF),
        vm((NQ, NX, rows, 3 * fs), BF),
        vm((NQ, rows, 3 * fs), F32),
        vm((NQ, 2, rows // 2, 3 * fs), F32),
        vm((NQ, 2, rows // 2, 3 * fs), BF),
        vm((NQ, 2, rows // 2, 3 * fs), BF),
        vm((NQ, 2, rows // 2, 3 * fs), BF),
        vm((NQ, 2, rows // 2, 3 * fs), BF),
        vm((NQ, 2, 2, rows // 2, 3 * fs), BF),
        vm((NQ, NR, rows, 3 * fs), BF),
        vm((rows, 2 * width), F32),
        vm((NE, blk, 2 * width), BF),
        vm((NE, blk, 2 * width), BF),
        vm((NR * tok, 2 * width), F32),
        vm((NR * tok, 128), F32),
        vm((NR, tok, 2 * width + 128), BF),
        vm((NR, tok, 2 * width + 128), BF),
        dma((17,)),
        dma((NR,)), dma((NR,)),
        dma((NE,)), dma((NE,)),
        dma((2,)),
        dma((NQ, NX)), dma((NQ, NX)),
        dma((NQ, 2)), dma((NQ, 2)),
        dma((NQ, 2)), dma((NQ, 2)),
        dma((NQ, 2)), dma((NQ, 2)),
        dma((NQ, NR)), dma((NQ, NR)),
        dma((NE,)), dma((NE,)),
        dma((NR,)), dma((NR,)),
        dma((NQ * NR + 1,)),
    ]
    vmem = pl.BlockSpec(memory_space=pltpu.VMEM)
    hbm = pl.BlockSpec(memory_space=pl.ANY)
    return pl.pallas_call(
        layer_kernel,
        name="layer",
        out_shape=(
            jax.ShapeDtypeStruct(tokens.shape, BF),
            jax.ShapeDtypeStruct(tokens.shape, BF),
            jax.ShapeDtypeStruct(routes.shape, F32),
            jax.ShapeDtypeStruct((NE, blk, 2 * width), BF),
            jax.ShapeDtypeStruct((NR, NQ * rows, 3 * fs), BF),
        ),
        in_specs=[vmem, vmem, vmem, vmem, hbm, hbm],
        out_specs=(vmem, vmem, vmem, hbm, hbm),
        scratch_shapes=scratch,
        compiler_params=pltpu.CompilerParams(
            collective_id=0, has_side_effects=True, vmem_limit_bytes=60 << 20
        ),
    )(tokens, cotangent, routes, gate_probs, w_gate_up, w_down)


def grads_kernel(rows_ref, act_ref, a_ref, b_ref, c_ref, gd_ref, ggu_hbm, a_out, b_out, c_out, xt, stg, sem):
    s = pl.program_id(0)
    slot = s % 2
    width = rows_ref.shape[1] // 2
    fs = gd_ref.shape[1]

    def out_copy(step, h):
        c = step * 2 + h
        return pltpu.make_async_copy(
            stg.at[step % 2, h],
            ggu_hbm.at[0, :, :, pl.ds(pl.multiple_of(c * 128, 128), 128)],
            sem.at[step % 2, h],
        )

    @pl.when(s >= 2)
    def _():
        for h in range(2):
            out_copy(s - 2, h).wait()

    @pl.when(s == 0)
    def _():
        a_out[...] = a_ref[...]
        b_out[...] = b_ref[...]
        c_out[...] = c_ref[...]
        xt[...] = rows_ref[:, 0:width].T

    act = act_ref[0]
    gd_ref[0] = dot_tn(act[:, 0:fs], rows_ref[:, width:]).astype(BF)
    pi = lax.broadcasted_iota(jnp.int32, (256, 256), 0)
    pj = lax.broadcasted_iota(jnp.int32, (256, 256), 1)
    perm = jnp.where(pi == jnp.where(pj < 128, 2 * pj, 2 * pj - 255), 1.0, 0.0).astype(BF)
    g = dot(xt[...], act[:, fs:]).astype(BF)
    for b in range(width // 128):
        gb = g[b * 128 : (b + 1) * 128]
        v = dot(perm, jnp.concatenate([gb[:, 0:fs], gb[:, fs:]], axis=0)).astype(BF)
        for h in range(2):
            stg.at[slot, h].reshape(2 * width, 128)[pl.ds(b * 256, 256), :] = v[:, h * 128 : (h + 1) * 128]
    for h in range(2):
        out_copy(s, h).start()

    @pl.when(s == pl.num_programs(0) - 1)
    def _():
        for h in range(2):
            out_copy(s - 1, h).wait()
        for h in range(2):
            out_copy(s, h).wait()


def weight_grads(rows, act, small, width, hid):
    fs = hid // NR
    n = rows.shape[0]
    return pl.pallas_call(
        grads_kernel,
        name="weight_grads",
        grid=(NR,),
        out_shape=(
            jax.ShapeDtypeStruct((1, hid, width), BF),
            jax.ShapeDtypeStruct((1, width, 2, hid), BF),
            *(jax.ShapeDtypeStruct(v.shape, v.dtype) for v in small),
        ),
        in_specs=[
            pl.BlockSpec((n, 2 * width), lambda s: (0, 0)),
            pl.BlockSpec((1, n, 3 * fs), lambda s: (s, 0, 0)),
            *(pl.BlockSpec(v.shape, lambda s: (0, 0)) for v in small),
        ],
        out_specs=(
            pl.BlockSpec((1, fs, width), lambda s: (0, s, 0)),
            pl.BlockSpec(memory_space=pl.ANY),
            *(pl.BlockSpec(v.shape, lambda s: (0, 0)) for v in small),
        ),
        scratch_shapes=[
            pltpu.VMEM((width, n), BF),
            pltpu.VMEM((2, 2, width, 2, 128), BF),
            pltpu.SemaphoreType.DMA((2, 2)),
        ],
        compiler_params=pltpu.CompilerParams(vmem_limit_bytes=60 << 20),
    )(rows, act, *small)


def on_device(tokens, routes, gate_probs, cotangent, w_gate_up, w_down):
    width, hid = w_gate_up.shape[1], w_gate_up.shape[3]
    layer_out, grad_tokens, dprob, rows, act = layer(
        tokens, cotangent, routes.T, gate_probs.T, w_gate_up, w_down
    )
    grad_down, grad_gate_up, layer_out, grad_tokens, dprob = weight_grads(
        rows.reshape(-1, 2 * width), act, (layer_out, grad_tokens, dprob), width, hid
    )
    return (layer_out, grad_tokens, dprob.T, grad_gate_up, grad_down)


def solution(mesh):
    rows = P(("erow", "ecol"), None)
    up, down = P("ecol", "erow", None, None), P("ecol", None, "erow")
    return jax.shard_map(
        on_device,
        mesh=mesh,
        in_specs=(rows, rows, rows, rows, up, down),
        out_specs=(rows, rows, rows, up, down),
        check_vma=False,
    )
```
